32 devices in a mesh: gx: 4 (over z), gy: 8 (over y, x, core).
Axes of the slice: x: 2, y: 2, z: 4, core: 2. Of those that a mesh axis runs over, the one named last changes fastest.
Arguments:
- adjoint_rhs: float32 [2, 3, 4, 512, 128], P(None, None, 'gx', 'gy'), may hold values from -6 to 6
- block_inverse: float32 [3, 3, 4, 512, 128], P(None, None, 'gx', 'gy'), may hold values from -0.3 to 1.3, as said below
- x_couplings: float32 [2, 3, 4, 512, 128], P(None, None, 'gx', 'gy'), may hold values from -0.8 to -0.3
- y_couplings: float32 [2, 3, 4, 512, 128], P(None, None, 'gx', 'gy'), may hold values from -0.3 to -0.05
- perf_cell: int32 [2048], P(('gx', 'gy')), may hold values from 0 to 8191
- perf_well: int32 [2048], P(('gx', 'gy')), may hold values from 0 to 127
- perf_weight: float32 [2048], P(('gx', 'gy')), may hold values from 0.5 to 2
- well_adjoint: float32 [3, 128], P(None, ('gx', 'gy')), may hold values from -6 to 6
Outputs:
- precond: float32 [2, 3, 4, 512, 128], P(None, None, 'gx', 'gy')
- well_update: float32 [3, 128], P(None, ('gx', 'gy'))
The draws below stay inside these ranges and needn't reach their ends.
Inputs may be any that keep to these rules, and one draw needn't show every extreme that they name: `perf_cell`: local cell index within the owning device's block. `block_inverse`: diagonal entries are at least 0.5, off-diagonal ones at most 0.3 in magnitude.
All inputs are finite; a program needn't handle non-finite values.
Results may differ from the reference program's by a relative error of at most 0.00017.
Values sent between devices are 32-bit elements; how exact they have to be, the bound alone decides.
A program may use at most 64 MiB of HBM per device.

```python
import math
import jax
import jax.numpy as jnp
import numpy as np
from jax import lax

NC = 3
PX = 1
CY = 64
CZ = 128
PERF_DEV = 64
NX = 4
NY = 512
NZ = 128
WELLS = 128
PERFS = 2048
N_GY = 8


def draw_block_inverse(key, part):
    uniform_values = jax.random.uniform(key, (NC, NC, NX, NY, NZ), jnp.float32)
    diagonal_mask = (jnp.arange(NC)[:, None] == jnp.arange(NC)[None, :])[:, :, None, None, None]
    diagonal = 0.6 + 0.6 * uniform_values
    offdiag = 0.25 * (2.0 * uniform_values - 1.0)
    return jnp.where(diagonal_mask, diagonal, offdiag)


def touch_ends(values, key, smallest, largest):
    place = [jax.random.randint(jax.random.fold_in(key, axis), (), 0, length) for axis, length in enumerate(values.shape)]
    widest = values.shape.index(max(values.shape))
    neighbour = place[:widest] + [(place[widest] + 1) % values.shape[widest]] + place[widest + 1:]
    return values.at[tuple(place)].set(smallest).at[tuple(neighbour)].set(largest)


def shard_levels(stream_key, shape, cuts, smallest, top_value):
    factor_of = 1.0
    for dim, parts in cuts:
        steps = jax.random.uniform(jax.random.fold_in(jax.random.fold_in(stream_key, 6), dim), (parts,), jnp.float32, smallest / len(cuts), top_value / len(cuts))
        factor_of = factor_of * jnp.repeat(jnp.exp(steps), shape[dim] // parts).reshape((-1,) + (1,) * (len(shape) - 1 - dim))
    return factor_of


def rank_bounds(count, lean):
    weights = [(1 << 20) // math.isqrt(grade ** lean) + 1 for grade in range(1, count + 1)]
    spread = 1 + sum(weights) // (1 << 30)
    return np.cumsum(np.array([max(1, weight // spread) for weight in weights]))


def ranked_ids(stream_key, shape, count, lean):
    table = rank_bounds(count, lean)
    pick = jax.random.randint(jax.random.fold_in(stream_key, 1), shape, 0, int(table[count - 1]))
    standing = jnp.searchsorted(jnp.asarray(table, jnp.int32), pick, side="right")
    return jax.random.permutation(jax.random.fold_in(stream_key, 2), count)[standing].astype(jnp.int32)


def noise(key, shape, scale, reach, cuts=(), held_as=jnp.bfloat16):
    values = scale * jax.random.normal(key, shape, jnp.float32)
    if cuts:
        values = values * shard_levels(key, shape, cuts, -0.22, 0.18)
    return jnp.clip(values, -reach, reach).astype(held_as)


def setup_inputs(seed: int = 0) -> dict:
    key_list = jax.random.split(jax.random.key(seed), 9)
    return {
        "adjoint_rhs": noise(key_list[0], (2, NC, NX, NY, NZ), 1.0, 6.0, ((2, 4), (3, 8)), jnp.float32),
        "block_inverse": draw_block_inverse(jax.random.fold_in(key_list[8], 71), 0),
        "x_couplings": jnp.clip(-0.8 + 0.5 * jax.random.uniform(key_list[2], (2, NC, NX, NY, NZ), jnp.float32) ** shard_levels(key_list[2], (2, NC, NX, NY, NZ), ((2, 4), (3, 8)), -0.2, 0.2), -0.8, -0.3),
        "y_couplings": jnp.clip(-0.3 + 0.25 * jax.random.uniform(key_list[3], (2, NC, NX, NY, NZ), jnp.float32) ** shard_levels(key_list[3], (2, NC, NX, NY, NZ), ((2, 4), (3, 8)), -0.2, 0.2), -0.3, -0.05),
        "perf_cell": touch_ends(jax.random.randint(key_list[4], (PERFS,), 0, PX * CY * CZ), jax.random.fold_in(key_list[4], 1), 0, (PX * CY * CZ) - 1).astype(jnp.int32),
        "perf_well": touch_ends(ranked_ids(key_list[5], (PERFS,), WELLS, 2), jax.random.fold_in(key_list[5], 3), 0, WELLS - 1).astype(jnp.int32),
        "perf_weight": jnp.clip(jnp.exp(math.log(2.0) - 1.3862944 * jax.random.uniform(key_list[6], (PERFS,), jnp.float32) ** shard_levels(key_list[6], (PERFS,), ((0, 32),), -0.2, 0.2)), 0.5, 2.0),
        "well_adjoint": noise(key_list[7], (NC, WELLS), 1.0, 6.0, ((1, 32),), jnp.float32),
    }


def apply_inverse(inverse, values):
    return inverse[:, 0] * values[None, 0] + inverse[:, 1] * values[None, 1] + inverse[:, 2] * values[None, 2]


def plane_apply(values, inverse, lower, upper):
    weighted = apply_inverse(inverse, values)
    border = jnp.zeros((weighted.shape[0], 1, weighted.shape[2]), jnp.float32)
    below = jnp.concatenate([border, weighted[:, :-1]], axis=1)
    above = jnp.concatenate([weighted[:, 1:], border], axis=1)
    return apply_inverse(inverse, values - lower * below - upper * above)


def factor_solve(rhs, inverse_t, x_low, x_up, y_low, y_up):
    rhs_t = jnp.moveaxis(rhs, 1, 0)

    def forward(previous, items):
        source, inverse, low, ylo, yup = items
        current = plane_apply(source - low * previous, inverse, ylo, yup)
        return current, current

    start = jnp.zeros(rhs_t.shape[1:], jnp.float32)
    _, forward_planes = lax.scan(forward, start, (rhs_t, inverse_t, x_low, y_low, y_up))

    def backward(following, items):
        current_q, inverse, high, ylo, yup = items
        current = current_q - plane_apply(high * following, inverse, ylo, yup)
        return current, current

    _, result = lax.scan(backward, start, (forward_planes, inverse_t, x_up, y_low, y_up), reverse=True)
    return jnp.moveaxis(result, 0, 1)


def reference(adjoint_rhs, block_inverse, x_couplings, y_couplings, perf_cell, perf_well, perf_weight, well_adjoint):
    device = (jnp.arange(PERFS) // PERF_DEV).astype(jnp.int32)
    block_x = device // N_GY
    block_y = device % N_GY
    plane = perf_cell // (CY * CZ)
    line = (perf_cell // CZ) % CY
    depth = perf_cell % CZ
    flat = ((block_x * PX + plane) * NY + block_y * CY + line) * NZ + depth
    flat = flat.astype(jnp.int32)
    terms = well_adjoint[:, perf_well] * perf_weight[None]
    source = jnp.zeros((NC, NX * NY * NZ), jnp.float32).at[:, flat].add(terms)
    source = source.reshape(NC, NX, NY, NZ)
    inverse_t = jnp.moveaxis(block_inverse, 2, 0)
    x_low = jnp.moveaxis(x_couplings[0], 1, 0)
    x_up = jnp.moveaxis(x_couplings[1], 1, 0)
    y_low = jnp.moveaxis(y_couplings[0], 1, 0)
    y_up = jnp.moveaxis(y_couplings[1], 1, 0)
    first = factor_solve(adjoint_rhs[0] + source, inverse_t, x_low, x_up, y_low, y_up)
    second = factor_solve(adjoint_rhs[1] + source, inverse_t, x_low, x_up, y_low, y_up)
    values = second.reshape(NC, NX * NY * NZ)[:, flat] * perf_weight[None]
    well_update = jax.ops.segment_sum(values.T, perf_well, num_segments=WELLS).T
    return jnp.stack([first, second]), well_update
```

```python
import functools

import jax
import jax.numpy as jnp
from jax import lax
from jax.experimental import pallas as pl
from jax.experimental.pallas import tpu as pltpu
from jax.sharding import PartitionSpec as P

MESH = pl.DeviceIdType.MESH
SUB = 8
LANES = 128
HIGHEST = lax.Precision.HIGHEST


def round_up(value, step):
    return -(-value // step) * step


def apply_inverse(inverse, values):
    comps = range(len(values))
    rows = []
    for c in comps:
        total = inverse[c][0] * values[0]
        for d in comps[1:]:
            total = total + inverse[c][d] * values[d]
        rows.append(total)
    return rows


def kernel(
    dims,
    rhs_h,
    inv_h,
    xc_h,
    yc_h,
    cell_ref,
    well_ref,
    weight_ref,
    adjoint_ref,
    out_ref,
    update_ref,
    rhs_s,
    inv_s,
    xc_s,
    yc_s,
    src_s,
    fwd_in,
    bwd_in,
    q_s,
    p_s,
    v_s,
    w_s,
    perf_s,
    ag1,
    ag2,
    rs1,
    rs2,
    load_sem,
    halo_send,
    halo_recv,
    ag1_send,
    ag1_recv,
    ag2_send,
    ag2_recv,
    rs1_send,
    rs1_recv,
    rs2_send,
    rs2_recv,
    fwd_send,
    fwd_recv,
    bwd_send,
    bwd_recv,
):
    n_gx, n_gy, ks, comps, inner, margin, depth, perfs, own_wells = dims
    groups = inner + 2 * margin
    a = lax.axis_index("gx")
    b = lax.axis_index("gy")

    loads = [
        pltpu.make_async_copy(src, dst.at[:, :, pl.ds(margin, inner)], load_sem.at[n])
        for n, (src, dst) in enumerate(
            ((rhs_h, rhs_s), (inv_h, inv_s), (xc_h, xc_s), (yc_h, yc_s))
        )
    ]
    for copy in loads:
        copy.start()

    barrier = pltpu.get_barrier_semaphore()
    for d in range(1, n_gy):
        pl.semaphore_signal(
            barrier, inc=1, device_id=(a, lax.rem(b + d, n_gy)), device_id_type=MESH
        )
    for d in range(1, n_gx):
        pl.semaphore_signal(
            barrier, inc=1, device_id=(lax.rem(a + d, n_gx), b), device_id_type=MESH
        )

    lane = lax.broadcasted_iota(jnp.int32, (comps, ag1.shape[2]), 1)
    first_well = (a * n_gy + b) * own_wells
    tile = jnp.zeros((comps, ag1.shape[2]), jnp.float32)
    for w in range(own_wells):
        tile = jnp.where(lane == first_well + w, adjoint_ref[:, w : w + 1], tile)
    ag1[0] = jnp.zeros(ag1.shape[1:], jnp.float32)
    ag1[0, 0:comps] = tile
    perf_s[0] = jnp.zeros(perf_s.shape[1:], jnp.float32)
    perf_s[0, 0:1, 0:perfs] = cell_ref[...].astype(jnp.float32)
    perf_s[0, 1:2, 0:perfs] = well_ref[...].astype(jnp.float32)
    perf_s[0, 2:3, 0:perfs] = weight_ref[...]

    zero_edges = ((0, b == 0, 0), (1, b == n_gy - 1, margin + inner))
    for side, missing, start in zero_edges:

        @pl.when(missing)
        def _():
            perf_s[1 + side] = jnp.zeros(perf_s.shape[1:], jnp.float32)
            for ref in (rhs_s, inv_s, xc_s, yc_s):
                ref[:, :, start : start + margin] = jnp.zeros(
                    ref.shape[:2] + (margin,) + ref.shape[3:], jnp.float32
                )

    edge = jnp.zeros((ks, comps, SUB, depth), jnp.float32)
    w_s[0] = edge
    w_s[groups + 1] = edge

    @pl.when(a == 0)
    def _():
        fwd_in[...] = jnp.zeros(fwd_in.shape, jnp.float32)

    pl.semaphore_wait(barrier, n_gy + n_gx - 2)

    def exchange(src, dst, send, recv, axis):
        size = n_gy if axis else n_gx
        copies = []
        for d in range(1, size):
            target = (a, lax.rem(b + d, n_gy)) if axis else (lax.rem(a + d, n_gx), b)
            copies.append(
                pltpu.make_async_remote_copy(
                    src_ref=src,
                    dst_ref=dst.at[d],
                    send_sem=send.at[d],
                    recv_sem=recv.at[d],
                    device_id=target,
                    device_id_type=MESH,
                )
            )
        for copy in copies:
            copy.start()
        return copies

    first = exchange(ag1.at[0], ag1, ag1_send, ag1_recv, 1)

    def halo(side):
        target = (a, b + 1) if side == 0 else (a, b - 1)
        start = inner - margin if side == 0 else 0
        place = 0 if side == 0 else margin + inner
        pairs = [(perf_s.at[0], perf_s.at[1 + side])]
        for src, dst in ((inv_h, inv_s), (rhs_h, rhs_s), (xc_h, xc_s), (yc_h, yc_s)):
            pairs.append(
                (src.at[:, :, pl.ds(start, margin)], dst.at[:, :, pl.ds(place, margin)])
            )
        return [
            pltpu.make_async_remote_copy(
                src_ref=src,
                dst_ref=dst,
                send_sem=halo_send.at[side, n],
                recv_sem=halo_recv.at[side, n],
                device_id=target,
                device_id_type=MESH,
            )
            for n, (src, dst) in enumerate(pairs)
        ]

    sends = ((0, b < n_gy - 1), (1, b > 0))
    receives = ((0, b > 0), (1, b < n_gy - 1))
    for side, present in sends:

        @pl.when(present)
        def _():
            for copy in halo(side):
                copy.start()

    for copy in first:
        copy.wait_recv()
    row = ag1[0]
    for d in range(1, n_gy):
        row = row + ag1[d]
    ag2[0] = row
    second = exchange(ag2.at[0], ag2, ag2_send, ag2_recv, 0)

    for copy in loads:
        copy.wait()
    for side, present in receives:

        @pl.when(present)
        def _():
            for copy in halo(side):
                copy.wait_recv()

    for copy in second:
        copy.wait_recv()
    wells = ag2[0]
    for d in range(1, n_gx):
        wells = wells + ag2[d]

    width = perf_s.shape[2]
    well_count = wells.shape[1]

    def perf_rows(slot):
        cell = perf_s[slot, 0:1].astype(jnp.int32)
        well = perf_s[slot, 1:2].astype(jnp.int32)
        line = lax.div(cell, depth)
        return line, cell - line * depth, well, perf_s[slot, 2:3]

    def well_hot(well):
        ids = lax.broadcasted_iota(jnp.int32, (well_count, width), 0)
        return (ids == well).astype(jnp.float32)

    def depth_hot(place):
        ids = lax.broadcasted_iota(jnp.int32, (depth, width), 0)
        return (ids == place).astype(jnp.float32)

    for slot, count, skip, start in (
        (0, inner, 0, margin),
        (1, margin, (inner - margin) * SUB, 0),
        (2, margin, 0, margin + inner),
    ):
        line, place, well, weight = perf_rows(slot)
        picked = jnp.dot(wells, well_hot(well), precision=HIGHEST)
        terms = picked * weight
        ids = lax.broadcasted_iota(jnp.int32, (count * SUB, width), 0) + skip
        hit = ids == line
        left = jnp.concatenate(
            [jnp.where(hit, terms[c : c + 1], 0.0) for c in range(comps)], axis=0
        )
        block = lax.dot_general(
            left, depth_hot(place), (((1,), (1,)), ((), ())), precision=HIGHEST
        )
        src_s[:, start : start + count] = block.reshape(comps, count, SUB, depth)

    sub = lax.broadcasted_iota(jnp.int32, (SUB, depth), 0)

    def load_inverse(g):
        return [[inv_s[c, d, g] for d in range(comps)] for c in range(comps)]

    def weigh(g, values):
        inverse = load_inverse(g)
        for k in range(ks):
            weighted = apply_inverse(inverse, values[k])
            for c in range(comps):
                v_s[g, k, c] = values[k][c]
                w_s[g + 1, k, c] = weighted[c]

    def solved(g):
        inverse = load_inverse(g)
        result = []
        for k in range(ks):
            rest = []
            for c in range(comps):
                here = w_s[g + 1, k, c]
                below = jnp.where(
                    sub == 0, pltpu.roll(w_s[g, k, c], 1, 0), pltpu.roll(here, 1, 0)
                )
                above = jnp.where(
                    sub == SUB - 1,
                    pltpu.roll(w_s[g + 2, k, c], SUB - 1, 0),
                    pltpu.roll(here, SUB - 1, 0),
                )
                rest.append(v_s[g, k, c] - yc_s[0, c, g] * below - yc_s[1, c, g] * above)
            result.append(apply_inverse(inverse, rest))
        return result

    def forward_copy(g):
        return pltpu.make_async_remote_copy(
            src_ref=q_s.at[g],
            dst_ref=fwd_in.at[g],
            send_sem=fwd_send.at[g],
            recv_sem=fwd_recv.at[g],
            device_id=(a + 1, b),
            device_id_type=MESH,
        )

    def turning_copy(g):
        return pltpu.make_async_remote_copy(
            src_ref=q_s.at[g],
            dst_ref=bwd_in.at[g],
            send_sem=bwd_send.at[g],
            recv_sem=bwd_recv.at[g],
            device_id=(a - 1, b),
            device_id_type=MESH,
        )

    def backward_copy(g):
        return pltpu.make_async_remote_copy(
            src_ref=p_s.at[g],
            dst_ref=bwd_in.at[g],
            send_sem=bwd_send.at[g],
            recv_sem=bwd_recv.at[g],
            device_id=(a - 1, b),
            device_id_type=MESH,
        )

    def forward_first(g):
        @pl.when(a > 0)
        def _():
            forward_copy(g).wait_recv()

        values = [
            [
                rhs_s[k, c, g] + src_s[c, g] - xc_s[0, c, g] * fwd_in[g, k, c]
                for c in range(comps)
            ]
            for k in range(ks)
        ]
        weigh(g, values)

    def forward_second(g):
        result = solved(g)
        for k in range(ks):
            for c in range(comps):
                q_s[g, k, c] = result[k][c]

        @pl.when(a < n_gx - 1)
        def _():
            forward_copy(g).start()

        if n_gx > 1:

            @pl.when(a == n_gx - 1)
            def _():
                turning_copy(g).start()

    def backward_first(g):
        backward_copy(g).wait_recv()
        values = [
            [xc_s[1, c, g] * bwd_in[g, k, c] for c in range(comps)] for k in range(ks)
        ]
        weigh(g, values)

    def backward_second(g):
        result = solved(g)
        for k in range(ks):
            for c in range(comps):
                p_s[g, k, c] = q_s[g, k, c] - result[k][c]

        @pl.when(a > 0)
        def _():
            backward_copy(g).start()

    def march(opening, closing):
        opening(0)

        def step(g, carry):
            opening(g)
            closing(g - 1)
            return carry

        lax.fori_loop(1, groups, step, 0)
        closing(groups - 1)

    march(forward_first, forward_second)

    @pl.when(a < n_gx - 1)
    def _():
        march(backward_first, backward_second)
        for k in range(ks):
            for c in range(comps):
                out_ref[k, c] = p_s[margin : margin + inner, k, c]

    @pl.when(a == n_gx - 1)
    def _():
        for k in range(ks):
            for c in range(comps):
                out_ref[k, c] = q_s[margin : margin + inner, k, c]

    line, place, well, weight = perf_rows(0)
    final = out_ref[ks - 1].reshape(comps * inner * SUB, depth)
    columns = jnp.dot(final, depth_hot(place), precision=HIGHEST)
    ids = lax.broadcasted_iota(jnp.int32, (inner * SUB, width), 0)
    hit = ids == line
    lines = inner * SUB
    sums = [
        jnp.sum(
            jnp.where(hit, columns[c * lines : (c + 1) * lines], 0.0), axis=0, keepdims=True
        )
        * weight
        for c in range(comps)
    ]
    sums.append(jnp.zeros((SUB - comps, width), jnp.float32))
    rs1[0] = lax.dot_general(
        jnp.concatenate(sums, axis=0),
        well_hot(well),
        (((1,), (1,)), ((), ())),
        precision=HIGHEST,
    )
    third = exchange(rs1.at[0], rs1, rs1_send, rs1_recv, 0)
    for copy in third:
        copy.wait_recv()
    column = rs1[0]
    for d in range(1, n_gx):
        column = column + rs1[d]
    rs2[0] = column
    fourth = exchange(rs2.at[0], rs2, rs2_send, rs2_recv, 1)

    for copy in first + second + third:
        copy.wait_send()
    for side, present in sends:

        @pl.when(present)
        def _():
            for copy in halo(side):
                copy.wait_send()

    def drain(make):
        def step(g, carry):
            make(g).wait_send()
            return carry

        lax.fori_loop(0, groups, step, 0)

    @pl.when(a < n_gx - 1)
    def _():
        drain(forward_copy)

    @pl.when(a > 0)
    def _():
        drain(backward_copy)

    for copy in fourth:
        copy.wait()
    total = rs2[0]
    for d in range(1, n_gy):
        total = total + rs2[d]
    total = total[0:comps]
    picked = [
        jnp.sum(jnp.where(lane == first_well + w, total, 0.0), axis=1, keepdims=True)
        for w in range(own_wells)
    ]
    update_ref[...] = jnp.concatenate(picked, axis=1)


def per_device(
    n_gx,
    n_gy,
    adjoint_rhs,
    block_inverse,
    x_couplings,
    y_couplings,
    perf_cell,
    perf_well,
    perf_weight,
    well_adjoint,
):
    ks, comps, planes, lines, depth = adjoint_rhs.shape
    assert planes == 1 and lines % SUB == 0
    inner = lines // SUB
    margin = round_up(2 * n_gx - 1, SUB) // SUB
    assert margin <= inner
    groups = inner + 2 * margin
    perfs = perf_cell.shape[0]
    own_wells = well_adjoint.shape[1]
    well_lanes = round_up(own_wells * n_gx * n_gy, LANES)
    perf_lanes = round_up(perfs, LANES)
    dims = (n_gx, n_gy, ks, comps, inner, margin, depth, perfs, own_wells)

    def grouped(array):
        return array.reshape(array.shape[:2] + (inner, SUB, depth))

    vmem = pl.BlockSpec(memory_space=pltpu.VMEM)
    hbm = pl.BlockSpec(memory_space=pl.ANY)
    f32 = jnp.float32
    dma = pltpu.SemaphoreType.DMA
    wide = lambda d0, d1: pltpu.VMEM((d0, d1, groups, SUB, depth), f32)
    flow = lambda extra: pltpu.VMEM((groups + extra, ks, comps, SUB, depth), f32)
    tiles = lambda count: pltpu.VMEM((count, SUB, well_lanes), f32)
    precond, update = pl.pallas_call(
        functools.partial(kernel, dims),
        out_shape=(
            jax.ShapeDtypeStruct((ks, comps, inner, SUB, depth), f32),
            jax.ShapeDtypeStruct((comps, own_wells), f32),
        ),
        in_specs=[hbm] * 4 + [vmem] * 4,
        out_specs=(vmem, vmem),
        scratch_shapes=[
            wide(ks, comps),
            wide(comps, comps),
            wide(2, comps),
            wide(2, comps),
            pltpu.VMEM((comps, groups, SUB, depth), f32),
            flow(0),
            flow(0),
            flow(0),
            flow(0),
            flow(0),
            flow(2),
            pltpu.VMEM((3, SUB, perf_lanes), f32),
            tiles(n_gy),
            tiles(n_gx),
            tiles(n_gx),
            tiles(n_gy),
            dma((4,)),
            dma((2, 5)),
            dma((2, 5)),
            dma((n_gy,)),
            dma((n_gy,)),
            dma((n_gx,)),
            dma((n_gx,)),
            dma((n_gx,)),
            dma((n_gx,)),
            dma((n_gy,)),
            dma((n_gy,)),
            dma((groups,)),
            dma((groups,)),
            dma((groups,)),
            dma((groups,)),
        ],
        compiler_params=pltpu.CompilerParams(collective_id=0, has_side_effects=True),
    )(
        grouped(adjoint_rhs),
        grouped(block_inverse),
        grouped(x_couplings),
        grouped(y_couplings),
        perf_cell.reshape(1, perfs),
        perf_well.reshape(1, perfs),
        perf_weight.reshape(1, perfs),
        well_adjoint,
    )
    return precond.reshape(adjoint_rhs.shape), update


def solution(mesh):
    placed = (
        P(None, None, "gx", "gy", None),
        P(None, None, "gx", "gy", None),
        P(None, None, "gx", "gy", None),
        P(None, None, "gx", "gy", None),
        P(("gx", "gy")),
        P(("gx", "gy")),
        P(("gx", "gy")),
        P(None, ("gx", "gy")),
    )
    return jax.shard_map(
        functools.partial(per_device, mesh.shape["gx"], mesh.shape["gy"]),
        mesh=mesh,
        in_specs=placed,
        out_specs=(P(None, None, "gx", "gy", None), P(None, ("gx", "gy"))),
        check_vma=False,
    )
```

```python
import functools

import jax
import jax.numpy as jnp
from jax import lax
from jax.experimental import pallas as pl
from jax.experimental.pallas import tpu as pltpu
from jax.sharding import PartitionSpec as P

MESH = pl.DeviceIdType.MESH
SUB = 8
LANES = 128
HIGHEST = lax.Precision.HIGHEST


def round_up(value, step):
    return -(-value // step) * step


def apply_inverse(inverse, values):
    comps = range(len(values))
    rows = []
    for c in comps:
        total = inverse[c][0] * values[0]
        for d in comps[1:]:
            total = total + inverse[c][d] * values[d]
        rows.append(total)
    return rows


def kernel(
    dims,
    rhs_h,
    inv_h,
    xc_h,
    yc_h,
    cell_ref,
    well_ref,
    weight_ref,
    adjoint_ref,
    out_ref,
    update_ref,
    rhs_s,
    inv_s,
    xc_s,
    yc_s,
    src_s,
    fwd_in,
    bwd_in,
    q_s,
    p_s,
    v_s,
    w_s,
    perf_s,
    ag1,
    ag2,
    rs1,
    rs2,
    well_hot,
    depth_hot,
    load_sem,
    halo_send,
    halo_recv,
    ag1_send,
    ag1_recv,
    ag2_send,
    ag2_recv,
    rs1_send,
    rs1_recv,
    rs2_send,
    rs2_recv,
    fwd_send,
    fwd_recv,
    bwd_send,
    bwd_recv,
):
    n_gx, n_gy, ks, comps, inner, margin, depth, perfs, own_wells = dims
    groups = inner + 2 * margin
    a = lax.axis_index("gx")
    b = lax.axis_index("gy")

    loads = [
        pltpu.make_async_copy(src, dst.at[:, :, pl.ds(margin, inner)], load_sem.at[n])
        for n, (src, dst) in enumerate(
            ((rhs_h, rhs_s), (inv_h, inv_s), (xc_h, xc_s), (yc_h, yc_s))
        )
    ]
    for copy in loads:
        copy.start()

    barrier = pltpu.get_barrier_semaphore()
    for d in range(1, n_gy):
        pl.semaphore_signal(
            barrier, inc=1, device_id=(a, lax.rem(b + d, n_gy)), device_id_type=MESH
        )
    for d in range(1, n_gx):
        pl.semaphore_signal(
            barrier, inc=1, device_id=(lax.rem(a + d, n_gx), b), device_id_type=MESH
        )

    lane = lax.broadcasted_iota(jnp.int32, (comps, ag1.shape[2]), 1)
    first_well = (a * n_gy + b) * own_wells
    tile = jnp.zeros((comps, ag1.shape[2]), jnp.float32)
    for w in range(own_wells):
        tile = jnp.where(lane == first_well + w, adjoint_ref[:, w : w + 1], tile)
    ag1[0] = jnp.zeros(ag1.shape[1:], jnp.float32)
    ag1[0, 0:comps] = tile
    perf_s[0] = jnp.zeros(perf_s.shape[1:], jnp.float32)
    perf_s[0, 0:1, 0:perfs] = cell_ref[...].astype(jnp.float32)
    perf_s[0, 1:2, 0:perfs] = well_ref[...].astype(jnp.float32)
    perf_s[0, 2:3, 0:perfs] = weight_ref[...]

    zero_edges = ((0, b == 0, 0), (1, b == n_gy - 1, margin + inner))
    for side, missing, start in zero_edges:

        @pl.when(missing)
        def _():
            perf_s[1 + side] = jnp.zeros(perf_s.shape[1:], jnp.float32)
            for ref in (rhs_s, inv_s, xc_s, yc_s):
                ref[:, :, start : start + margin] = jnp.zeros(
                    ref.shape[:2] + (margin,) + ref.shape[3:], jnp.float32
                )

    edge = jnp.zeros((ks, comps, SUB, depth), jnp.float32)
    w_s[:, 0] = edge
    w_s[:, groups + 1] = edge

    @pl.when(a == 0)
    def _():
        fwd_in[...] = jnp.zeros(fwd_in.shape, jnp.float32)

    pl.semaphore_wait(barrier, n_gy + n_gx - 2)

    def exchanged(src, dst, send, recv, axis):
        size = n_gy if axis else n_gx
        copies = []
        for d in range(1, size):
            target = (a, lax.rem(b + d, n_gy)) if axis else (lax.rem(a + d, n_gx), b)
            copies.append(
                pltpu.make_async_remote_copy(
                    src_ref=src,
                    dst_ref=dst.at[d],
                    send_sem=send.at[d],
                    recv_sem=recv.at[d],
                    device_id=target,
                    device_id_type=MESH,
                )
            )
        return copies

    def exchange(*args):
        copies = exchanged(*args)
        for copy in copies:
            copy.start()
        return copies

    first = exchange(ag1.at[0], ag1, ag1_send, ag1_recv, 1)

    def halo(side):
        target = (a, b + 1) if side == 0 else (a, b - 1)
        start = inner - margin if side == 0 else 0
        place = 0 if side == 0 else margin + inner
        pairs = [(perf_s.at[0], perf_s.at[1 + side])]
        for src, dst in ((inv_h, inv_s), (rhs_h, rhs_s), (xc_h, xc_s), (yc_h, yc_s)):
            pairs.append(
                (src.at[:, :, pl.ds(start, margin)], dst.at[:, :, pl.ds(place, margin)])
            )
        return [
            pltpu.make_async_remote_copy(
                src_ref=src,
                dst_ref=dst,
                send_sem=halo_send.at[side, n],
                recv_sem=halo_recv.at[side, n],
                device_id=target,
                device_id_type=MESH,
            )
            for n, (src, dst) in enumerate(pairs)
        ]

    sends = ((0, b < n_gy - 1), (1, b > 0))
    receives = ((0, b > 0), (1, b < n_gy - 1))
    for side, present in sends:

        @pl.when(present)
        def _():
            for copy in halo(side):
                copy.start()

    width = perf_s.shape[2]
    well_count = ag1.shape[2]

    def perf_rows(slot):
        cell = perf_s[slot, 0:1].astype(jnp.int32)
        well = perf_s[slot, 1:2].astype(jnp.int32)
        line = lax.div(cell, depth)
        return line, cell - line * depth, well, perf_s[slot, 2:3]

    def make_hot(slot):
        _, place, well, _ = perf_rows(slot)
        ids = lax.broadcasted_iota(jnp.int32, (well_count, width), 0)
        well_hot[slot] = (ids == well).astype(jnp.float32)
        ids = lax.broadcasted_iota(jnp.int32, (depth, width), 0)
        depth_hot[slot] = (ids == place).astype(jnp.float32)

    make_hot(0)

    for copy in first:
        copy.wait_recv()
    row = ag1[0]
    for d in range(1, n_gy):
        row = row + ag1[d]
    ag2[0] = row
    second = exchange(ag2.at[0], ag2, ag2_send, ag2_recv, 0)

    for copy in loads:
        copy.wait()
    for side, present in receives:

        @pl.when(present)
        def _():
            for copy in halo(side):
                copy.wait_recv()

    make_hot(1)
    make_hot(2)
    for copy in second:
        copy.wait_recv()
    wells = ag2[0]
    for d in range(1, n_gx):
        wells = wells + ag2[d]

    for slot, count, skip, start in (
        (0, inner, 0, margin),
        (1, margin, (inner - margin) * SUB, 0),
        (2, margin, 0, margin + inner),
    ):
        line, _, _, weight = perf_rows(slot)
        picked = jnp.dot(wells, well_hot[slot], precision=HIGHEST)
        terms = picked * weight
        ids = lax.broadcasted_iota(jnp.int32, (count * SUB, width), 0) + skip
        hit = ids == line
        left = jnp.concatenate(
            [jnp.where(hit, terms[c : c + 1], 0.0) for c in range(comps)], axis=0
        )
        block = lax.dot_general(
            left, depth_hot[slot], (((1,), (1,)), ((), ())), precision=HIGHEST
        )
        src_s[:, start : start + count] = block.reshape(comps, count, SUB, depth)

    sub = lax.broadcasted_iota(jnp.int32, (SUB, depth), 0)

    def load_inverse(g):
        return [[inv_s[c, d, g] for d in range(comps)] for c in range(comps)]

    def weigh(k, g, values):
        weighted = apply_inverse(load_inverse(g), values)
        for c in range(comps):
            v_s[k, g, c] = values[c]
            w_s[k, g + 1, c] = weighted[c]

    def solved(k, g):
        rest = []
        for c in range(comps):
            here = w_s[k, g + 1, c]
            below = jnp.where(
                sub == 0, pltpu.roll(w_s[k, g, c], 1, 0), pltpu.roll(here, 1, 0)
            )
            above = jnp.where(
                sub == SUB - 1,
                pltpu.roll(w_s[k, g + 2, c], SUB - 1, 0),
                pltpu.roll(here, SUB - 1, 0),
            )
            rest.append(v_s[k, g, c] - yc_s[0, c, g] * below - yc_s[1, c, g] * above)
        return apply_inverse(load_inverse(g), rest)

    def forward_copy(k, g):
        return pltpu.make_async_remote_copy(
            src_ref=q_s.at[k, g],
            dst_ref=fwd_in.at[k, g],
            send_sem=fwd_send.at[k, g],
            recv_sem=fwd_recv.at[k, g],
            device_id=(a + 1, b),
            device_id_type=MESH,
        )

    def backward_copy(k, g, src):
        return pltpu.make_async_remote_copy(
            src_ref=src.at[k, g],
            dst_ref=bwd_in.at[k, g],
            send_sem=bwd_send.at[k, g],
            recv_sem=bwd_recv.at[k, g],
            device_id=(a - 1, b),
            device_id_type=MESH,
        )

    def forward_first(k, g):
        @pl.when(a > 0)
        def _():
            forward_copy(k, g).wait_recv()

        weigh(
            k,
            g,
            [
                rhs_s[k, c, g] + src_s[c, g] - xc_s[0, c, g] * fwd_in[k, g, c]
                for c in range(comps)
            ],
        )

    def forward_second(k, g):
        result = solved(k, g)
        for c in range(comps):
            q_s[k, g, c] = result[c]

        @pl.when(a < n_gx - 1)
        def _():
            forward_copy(k, g).start()

        @pl.when(a == n_gx - 1)
        def _():
            backward_copy(k, g, q_s).start()

    def backward_first(k, g):
        backward_copy(k, g, p_s).wait_recv()
        weigh(k, g, [xc_s[1, c, g] * bwd_in[k, g, c] for c in range(comps)])

    def backward_second(k, g):
        result = solved(k, g)
        for c in range(comps):
            p_s[k, g, c] = q_s[k, g, c] - result[c]

        @pl.when(a > 0)
        def _():
            backward_copy(k, g, p_s).start()

    def march(k, opening, closing):
        opening(k, 0)

        def step(g, carry):
            opening(k, g)
            closing(k, g - 1)
            return carry

        lax.fori_loop(1, groups, step, 0)
        closing(k, groups - 1)

    def deliver(k, source):
        for c in range(comps):
            out_ref[k, c] = source[k, margin : margin + inner, c]

    def well_sums():
        line, _, _, weight = perf_rows(0)
        lines = inner * SUB
        final = out_ref[ks - 1].reshape(comps * lines, depth)
        columns = jnp.dot(final, depth_hot[0], precision=HIGHEST)
        ids = lax.broadcasted_iota(jnp.int32, (lines, width), 0)
        hit = ids == line
        sums = [
            jnp.sum(
                jnp.where(hit, columns[c * lines : (c + 1) * lines], 0.0),
                axis=0,
                keepdims=True,
            )
            * weight
            for c in range(comps)
        ]
        sums.append(jnp.zeros((SUB - comps, width), jnp.float32))
        rs1[0] = lax.dot_general(
            jnp.concatenate(sums, axis=0),
            well_hot[0],
            (((1,), (1,)), ((), ())),
            precision=HIGHEST,
        )
        for copy in exchanged(rs1.at[0], rs1, rs1_send, rs1_recv, 0):
            copy.start()

    order = range(ks - 1, -1, -1)
    for k in order:
        march(k, forward_first, forward_second)

    @pl.when(a == n_gx - 1)
    def _():
        for k in order:
            deliver(k, q_s)

    @pl.when(a < n_gx - 1)
    def _():
        march(ks - 1, backward_first, backward_second)
        deliver(ks - 1, p_s)

    @pl.when(a == 0)
    def _():
        well_sums()

    @pl.when(a < n_gx - 1)
    def _():
        for k in order[1:]:
            march(k, backward_first, backward_second)
            deliver(k, p_s)

    @pl.when(a > 0)
    def _():
        well_sums()

    third = exchanged(rs1.at[0], rs1, rs1_send, rs1_recv, 0)
    for copy in third:
        copy.wait_recv()
    column = rs1[0]
    for d in range(1, n_gx):
        column = column + rs1[d]
    rs2[0] = column
    fourth = exchange(rs2.at[0], rs2, rs2_send, rs2_recv, 1)

    for copy in first + second + third:
        copy.wait_send()
    for side, present in sends:

        @pl.when(present)
        def _():
            for copy in halo(side):
                copy.wait_send()

    def drain(make):
        for k in range(ks):

            def step(g, carry):
                make(k, g).wait_send()
                return carry

            lax.fori_loop(0, groups, step, 0)

    @pl.when(a < n_gx - 1)
    def _():
        drain(forward_copy)

    @pl.when(a > 0)
    def _():
        drain(lambda k, g: backward_copy(k, g, p_s))

    for copy in fourth:
        copy.wait()
    total = rs2[0]
    for d in range(1, n_gy):
        total = total + rs2[d]
    total = total[0:comps]
    picked = [
        jnp.sum(jnp.where(lane == first_well + w, total, 0.0), axis=1, keepdims=True)
        for w in range(own_wells)
    ]
    update_ref[...] = jnp.concatenate(picked, axis=1)


def per_device(
    n_gx,
    n_gy,
    adjoint_rhs,
    block_inverse,
    x_couplings,
    y_couplings,
    perf_cell,
    perf_well,
    perf_weight,
    well_adjoint,
):
    ks, comps, planes, lines, depth = adjoint_rhs.shape
    assert planes == 1 and n_gx > 1 and lines % SUB == 0
    inner = lines // SUB
    margin = round_up(2 * n_gx - 1, SUB) // SUB
    assert margin <= inner
    groups = inner + 2 * margin
    perfs = perf_cell.shape[0]
    own_wells = well_adjoint.shape[1]
    well_lanes = round_up(own_wells * n_gx * n_gy, LANES)
    perf_lanes = round_up(perfs, LANES)
    dims = (n_gx, n_gy, ks, comps, inner, margin, depth, perfs, own_wells)

    def grouped(array):
        return array.reshape(array.shape[:2] + (inner, SUB, depth))

    vmem = pl.BlockSpec(memory_space=pltpu.VMEM)
    hbm = pl.BlockSpec(memory_space=pl.ANY)
    f32 = jnp.float32
    dma = pltpu.SemaphoreType.DMA
    wide = lambda d0, d1: pltpu.VMEM((d0, d1, groups, SUB, depth), f32)
    flow = lambda extra: pltpu.VMEM((ks, groups + extra, comps, SUB, depth), f32)
    tiles = lambda count: pltpu.VMEM((count, SUB, well_lanes), f32)
    precond, update = pl.pallas_call(
        functools.partial(kernel, dims),
        out_shape=(
            pltpu.VMEM((ks, comps, inner, SUB, depth), f32),
            pltpu.VMEM((comps, own_wells), f32),
        ),
        in_specs=[hbm] * 4 + [vmem] * 4,
        out_specs=(vmem, vmem),
        scratch_shapes=[
            wide(ks, comps),
            wide(comps, comps),
            wide(2, comps),
            wide(2, comps),
            pltpu.VMEM((comps, groups, SUB, depth), f32),
            flow(0),
            flow(0),
            flow(0),
            flow(0),
            flow(0),
            flow(2),
            pltpu.VMEM((3, SUB, perf_lanes), f32),
            tiles(n_gy),
            tiles(n_gx),
            tiles(n_gx),
            tiles(n_gy),
            pltpu.VMEM((3, well_lanes, perf_lanes), f32),
            pltpu.VMEM((3, depth, perf_lanes), f32),
            dma((4,)),
            dma((2, 5)),
            dma((2, 5)),
            dma((n_gy,)),
            dma((n_gy,)),
            dma((n_gx,)),
            dma((n_gx,)),
            dma((n_gx,)),
            dma((n_gx,)),
            dma((n_gy,)),
            dma((n_gy,)),
            dma((ks, groups)),
            dma((ks, groups)),
            dma((ks, groups)),
            dma((ks, groups)),
        ],
        compiler_params=pltpu.CompilerParams(collective_id=0, has_side_effects=True),
    )(
        grouped(adjoint_rhs),
        grouped(block_inverse),
        grouped(x_couplings),
        grouped(y_couplings),
        perf_cell.reshape(1, perfs),
        perf_well.reshape(1, perfs),
        perf_weight.reshape(1, perfs),
        well_adjoint,
    )
    return precond.reshape(adjoint_rhs.shape), update


def solution(mesh):
    placed = (
        P(None, None, "gx", "gy", None),
        P(None, None, "gx", "gy", None),
        P(None, None, "gx", "gy", None),
        P(None, None, "gx", "gy", None),
        P(("gx", "gy")),
        P(("gx", "gy")),
        P(("gx", "gy")),
        P(None, ("gx", "gy")),
    )
    return jax.shard_map(
        functools.partial(per_device, mesh.shape["gx"], mesh.shape["gy"]),
        mesh=mesh,
        in_specs=placed,
        out_specs=(P(None, None, "gx", "gy", None), P(None, ("gx", "gy"))),
        check_vma=False,
    )
```

```python
import functools

import jax
import jax.numpy as jnp
from jax import lax
from jax.experimental import pallas as pl
from jax.experimental.pallas import tpu as pltpu
from jax.sharding import PartitionSpec as P

MESH = pl.DeviceIdType.MESH
SUB = 8
LANES = 128


def round_up(value, step):
    return -(-value // step) * step


def dot_exact(values, hot, contract):
    rows = values.shape[0]
    high = values.astype(jnp.bfloat16)
    rest = values - high.astype(jnp.float32)
    middle = rest.astype(jnp.bfloat16)
    low = (rest - middle.astype(jnp.float32)).astype(jnp.bfloat16)
    dims = (((1,), (contract,)), ((), ()))
    return sum(
        lax.dot_general(part, hot, dims, preferred_element_type=jnp.float32)
        for part in (low, middle, high)
    )


def apply_inverse(inverse, values):
    comps = range(len(values))
    rows = []
    for c in comps:
        total = inverse[c][0] * values[0]
        for d in comps[1:]:
            total = total + inverse[c][d] * values[d]
        rows.append(total)
    return rows


def kernel(
    dims,
    rhs_h,
    inv_h,
    xc_h,
    yc_h,
    cell_ref,
    well_ref,
    weight_ref,
    adjoint_ref,
    out_ref,
    update_ref,
    rhs_s,
    inv_s,
    xc_s,
    yc_s,
    src_s,
    fwd_in,
    bwd_in,
    q_s,
    p_s,
    v_s,
    w_s,
    perf_s,
    ag1,
    ag2,
    rs1,
    rs2,
    well_hot,
    depth_hot,
    load_sem,
    halo_send,
    halo_recv,
    ag1_send,
    ag1_recv,
    ag2_send,
    ag2_recv,
    rs1_send,
    rs1_recv,
    rs2_send,
    rs2_recv,
    fwd_send,
    fwd_recv,
    bwd_send,
    bwd_recv,
):
    n_gx, n_gy, ks, comps, inner, margin, depth, perfs, own_wells = dims
    groups = inner + 2 * margin
    a = lax.axis_index("gx")
    b = lax.axis_index("gy")

    loads = [
        pltpu.make_async_copy(src, dst.at[:, :, pl.ds(margin, inner)], load_sem.at[n])
        for n, (src, dst) in enumerate(
            ((rhs_h, rhs_s), (inv_h, inv_s), (xc_h, xc_s), (yc_h, yc_s))
        )
    ]
    for copy in loads:
        copy.start()

    barrier = pltpu.get_barrier_semaphore()
    for d in range(1, n_gy):
        pl.semaphore_signal(
            barrier, inc=1, device_id=(a, lax.rem(b + d, n_gy)), device_id_type=MESH
        )
    for d in range(1, n_gx):
        pl.semaphore_signal(
            barrier, inc=1, device_id=(lax.rem(a + d, n_gx), b), device_id_type=MESH
        )

    lane = lax.broadcasted_iota(jnp.int32, (comps, ag1.shape[2]), 1)
    first_well = (a * n_gy + b) * own_wells
    tile = jnp.zeros((comps, ag1.shape[2]), jnp.float32)
    for w in range(own_wells):
        tile = jnp.where(lane == first_well + w, adjoint_ref[:, w : w + 1], tile)
    ag1[0] = jnp.zeros(ag1.shape[1:], jnp.float32)
    ag1[0, 0:comps] = tile
    perf_s[0] = jnp.zeros(perf_s.shape[1:], jnp.float32)
    perf_s[0, 0:1, 0:perfs] = cell_ref[...].astype(jnp.float32)
    perf_s[0, 1:2, 0:perfs] = well_ref[...].astype(jnp.float32)
    perf_s[0, 2:3, 0:perfs] = weight_ref[...]

    zero_edges = ((0, b == 0, 0), (1, b == n_gy - 1, margin + inner))
    for side, missing, start in zero_edges:

        @pl.when(missing)
        def _():
            perf_s[1 + side] = jnp.zeros(perf_s.shape[1:], jnp.float32)
            for ref in (rhs_s, inv_s, xc_s, yc_s):
                ref[:, :, start : start + margin] = jnp.zeros(
                    ref.shape[:2] + (margin,) + ref.shape[3:], jnp.float32
                )

    edge = jnp.zeros((ks, comps, SUB, depth), jnp.float32)
    w_s[:, 0] = edge
    w_s[:, groups + 1] = edge

    @pl.when(a == 0)
    def _():
        fwd_in[...] = jnp.zeros(fwd_in.shape, jnp.float32)

    pl.semaphore_wait(barrier, n_gy + n_gx - 2)

    def exchanged(src, dst, send, recv, axis):
        size = n_gy if axis else n_gx
        copies = []
        for d in range(1, size):
            target = (a, lax.rem(b + d, n_gy)) if axis else (lax.rem(a + d, n_gx), b)
            copies.append(
                pltpu.make_async_remote_copy(
                    src_ref=src,
                    dst_ref=dst.at[d],
                    send_sem=send.at[d],
                    recv_sem=recv.at[d],
                    device_id=target,
                    device_id_type=MESH,
                )
            )
        return copies

    def exchange(*args):
        copies = exchanged(*args)
        for copy in copies:
            copy.start()
        return copies

    first = exchange(ag1.at[0], ag1, ag1_send, ag1_recv, 1)

    def halo(side):
        target = (a, b + 1) if side == 0 else (a, b - 1)
        start = inner - margin if side == 0 else 0
        place = 0 if side == 0 else margin + inner
        pairs = [(perf_s.at[0], perf_s.at[1 + side])]
        for src, dst in ((inv_h, inv_s), (rhs_h, rhs_s), (xc_h, xc_s), (yc_h, yc_s)):
            pairs.append(
                (src.at[:, :, pl.ds(start, margin)], dst.at[:, :, pl.ds(place, margin)])
            )
        return [
            pltpu.make_async_remote_copy(
                src_ref=src,
                dst_ref=dst,
                send_sem=halo_send.at[side, n],
                recv_sem=halo_recv.at[side, n],
                device_id=target,
                device_id_type=MESH,
            )
            for n, (src, dst) in enumerate(pairs)
        ]

    sends = ((0, b < n_gy - 1), (1, b > 0))
    receives = ((0, b > 0), (1, b < n_gy - 1))
    for side, present in sends:

        @pl.when(present)
        def _():
            for copy in halo(side):
                copy.start()

    width = perf_s.shape[2]
    well_count = ag1.shape[2]

    def perf_rows(slot):
        cell = perf_s[slot, 0:1].astype(jnp.int32)
        well = perf_s[slot, 1:2].astype(jnp.int32)
        line = lax.div(cell, depth)
        return line, cell - line * depth, well, perf_s[slot, 2:3]

    def make_hot(slot):
        _, place, well, _ = perf_rows(slot)
        ids = lax.broadcasted_iota(jnp.int32, (well_count, width), 0)
        well_hot[slot] = (ids == well).astype(jnp.float32).astype(jnp.bfloat16)
        ids = lax.broadcasted_iota(jnp.int32, (depth, width), 0)
        depth_hot[slot] = (ids == place).astype(jnp.float32).astype(jnp.bfloat16)

    make_hot(0)

    for copy in first:
        copy.wait_recv()
    row = ag1[0]
    for d in range(1, n_gy):
        row = row + ag1[d]
    ag2[0] = row
    second = exchange(ag2.at[0], ag2, ag2_send, ag2_recv, 0)

    for copy in loads:
        copy.wait()
    for side, present in receives:

        @pl.when(present)
        def _():
            for copy in halo(side):
                copy.wait_recv()

    make_hot(1)
    make_hot(2)
    for copy in second:
        copy.wait_recv()
    wells = ag2[0]
    for d in range(1, n_gx):
        wells = wells + ag2[d]

    for slot, count, skip, start in (
        (0, inner, 0, margin),
        (1, margin, (inner - margin) * SUB, 0),
        (2, margin, 0, margin + inner),
    ):
        line, _, _, weight = perf_rows(slot)
        picked = dot_exact(wells, well_hot[slot], 0)
        terms = picked * weight
        ids = lax.broadcasted_iota(jnp.int32, (count * SUB, width), 0) + skip
        hit = ids == line
        left = jnp.concatenate(
            [jnp.where(hit, terms[c : c + 1], 0.0) for c in range(comps)], axis=0
        )
        block = dot_exact(left, depth_hot[slot], 1)
        src_s[:, start : start + count] = block.reshape(comps, count, SUB, depth)

    sub = lax.broadcasted_iota(jnp.int32, (SUB, depth), 0)

    def load_inverse(g):
        return [[inv_s[c, d, g] for d in range(comps)] for c in range(comps)]

    def weigh(k, g, values):
        weighted = apply_inverse(load_inverse(g), values)
        for c in range(comps):
            v_s[k, g, c] = values[c]
            w_s[k, g + 1, c] = weighted[c]

    def solved(k, g):
        rest = []
        for c in range(comps):
            here = w_s[k, g + 1, c]
            below = jnp.where(
                sub == 0, pltpu.roll(w_s[k, g, c], 1, 0), pltpu.roll(here, 1, 0)
            )
            above = jnp.where(
                sub == SUB - 1,
                pltpu.roll(w_s[k, g + 2, c], SUB - 1, 0),
                pltpu.roll(here, SUB - 1, 0),
            )
            rest.append(v_s[k, g, c] - yc_s[0, c, g] * below - yc_s[1, c, g] * above)
        return apply_inverse(load_inverse(g), rest)

    def forward_copy(k, g):
        return pltpu.make_async_remote_copy(
            src_ref=q_s.at[k, g],
            dst_ref=fwd_in.at[k, g],
            send_sem=fwd_send.at[k, g],
            recv_sem=fwd_recv.at[k, g],
            device_id=(a + 1, b),
            device_id_type=MESH,
        )

    def backward_copy(k, g, src):
        return pltpu.make_async_remote_copy(
            src_ref=src.at[k, g],
            dst_ref=bwd_in.at[k, g],
            send_sem=bwd_send.at[k, g],
            recv_sem=bwd_recv.at[k, g],
            device_id=(a - 1, b),
            device_id_type=MESH,
        )

    def forward_first(k, g):
        @pl.when(a > 0)
        def _():
            forward_copy(k, g).wait_recv()

        weigh(
            k,
            g,
            [
                rhs_s[k, c, g] + src_s[c, g] - xc_s[0, c, g] * fwd_in[k, g, c]
                for c in range(comps)
            ],
        )

    def forward_second(k, g):
        result = solved(k, g)
        for c in range(comps):
            q_s[k, g, c] = result[c]

        @pl.when(a < n_gx - 1)
        def _():
            forward_copy(k, g).start()

        @pl.when(a == n_gx - 1)
        def _():
            backward_copy(k, g, q_s).start()

    def backward_first(k, g):
        backward_copy(k, g, p_s).wait_recv()
        weigh(k, g, [xc_s[1, c, g] * bwd_in[k, g, c] for c in range(comps)])

    def backward_second(k, g):
        result = solved(k, g)
        for c in range(comps):
            p_s[k, g, c] = q_s[k, g, c] - result[c]

        @pl.when(a > 0)
        def _():
            backward_copy(k, g, p_s).start()

    def march(k, opening, closing):
        opening(k, 0)

        def step(g, carry):
            opening(k, g)
            closing(k, g - 1)
            return carry

        lax.fori_loop(1, groups, step, 0)
        closing(k, groups - 1)

    def deliver(k, source):
        for c in range(comps):
            out_ref[k, c] = source[k, margin : margin + inner, c]

    def well_sums():
        line, _, _, weight = perf_rows(0)
        lines = inner * SUB
        final = out_ref[ks - 1].reshape(comps * lines, depth)
        columns = dot_exact(final, depth_hot[0], 0)
        ids = lax.broadcasted_iota(jnp.int32, (lines, width), 0)
        hit = ids == line
        sums = [
            jnp.sum(
                jnp.where(hit, columns[c * lines : (c + 1) * lines], 0.0),
                axis=0,
                keepdims=True,
            )
            * weight
            for c in range(comps)
        ]
        sums.append(jnp.zeros((SUB - comps, width), jnp.float32))
        rs1[0] = dot_exact(jnp.concatenate(sums, axis=0), well_hot[0], 1)
        for copy in exchanged(rs1.at[0], rs1, rs1_send, rs1_recv, 0):
            copy.start()

    order = range(ks - 1, -1, -1)
    for k in order:
        march(k, forward_first, forward_second)

    @pl.when(a == n_gx - 1)
    def _():
        for k in order:
            deliver(k, q_s)

    @pl.when(a < n_gx - 1)
    def _():
        march(ks - 1, backward_first, backward_second)
        deliver(ks - 1, p_s)

    @pl.when(a == 0)
    def _():
        well_sums()

    @pl.when(a < n_gx - 1)
    def _():
        for k in order[1:]:
            march(k, backward_first, backward_second)
            deliver(k, p_s)

    @pl.when(a > 0)
    def _():
        well_sums()

    third = exchanged(rs1.at[0], rs1, rs1_send, rs1_recv, 0)
    for copy in third:
        copy.wait_recv()
    column = rs1[0]
    for d in range(1, n_gx):
        column = column + rs1[d]
    rs2[0] = column
    fourth = exchange(rs2.at[0], rs2, rs2_send, rs2_recv, 1)

    for copy in first + second + third:
        copy.wait_send()
    for side, present in sends:

        @pl.when(present)
        def _():
            for copy in halo(side):
                copy.wait_send()

    def drain(make):
        for k in range(ks):

            def step(g, carry):
                make(k, g).wait_send()
                return carry

            lax.fori_loop(0, groups, step, 0)

    @pl.when(a < n_gx - 1)
    def _():
        drain(forward_copy)

    @pl.when(a > 0)
    def _():
        drain(lambda k, g: backward_copy(k, g, p_s))

    for copy in fourth:
        copy.wait()
    total = rs2[0]
    for d in range(1, n_gy):
        total = total + rs2[d]
    total = total[0:comps]
    picked = [
        jnp.sum(jnp.where(lane == first_well + w, total, 0.0), axis=1, keepdims=True)
        for w in range(own_wells)
    ]
    update_ref[...] = jnp.concatenate(picked, axis=1)


def per_device(
    n_gx,
    n_gy,
    adjoint_rhs,
    block_inverse,
    x_couplings,
    y_couplings,
    perf_cell,
    perf_well,
    perf_weight,
    well_adjoint,
):
    ks, comps, planes, lines, depth = adjoint_rhs.shape
    assert planes == 1 and n_gx > 1 and lines % SUB == 0
    inner = lines // SUB
    margin = round_up(2 * n_gx - 1, SUB) // SUB
    assert margin <= inner
    groups = inner + 2 * margin
    perfs = perf_cell.shape[0]
    own_wells = well_adjoint.shape[1]
    well_lanes = round_up(own_wells * n_gx * n_gy, LANES)
    perf_lanes = round_up(perfs, LANES)
    dims = (n_gx, n_gy, ks, comps, inner, margin, depth, perfs, own_wells)

    def grouped(array):
        return array.reshape(array.shape[:2] + (inner, SUB, depth))

    vmem = pl.BlockSpec(memory_space=pltpu.VMEM)
    hbm = pl.BlockSpec(memory_space=pl.ANY)
    f32 = jnp.float32
    dma = pltpu.SemaphoreType.DMA
    wide = lambda d0, d1: pltpu.VMEM((d0, d1, groups, SUB, depth), f32)
    flow = lambda extra: pltpu.VMEM((ks, groups + extra, comps, SUB, depth), f32)
    tiles = lambda count: pltpu.VMEM((count, SUB, well_lanes), f32)
    precond, update = pl.pallas_call(
        functools.partial(kernel, dims),
        out_shape=(
            pltpu.VMEM((ks, comps, inner, SUB, depth), f32),
            pltpu.VMEM((comps, own_wells), f32),
        ),
        in_specs=[hbm] * 4 + [vmem] * 4,
        out_specs=(vmem, vmem),
        scratch_shapes=[
            wide(ks, comps),
            wide(comps, comps),
            wide(2, comps),
            wide(2, comps),
            pltpu.VMEM((comps, groups, SUB, depth), f32),
            flow(0),
            flow(0),
            flow(0),
            flow(0),
            flow(0),
            flow(2),
            pltpu.VMEM((3, SUB, perf_lanes), f32),
            tiles(n_gy),
            tiles(n_gx),
            tiles(n_gx),
            tiles(n_gy),
            pltpu.VMEM((3, well_lanes, perf_lanes), jnp.bfloat16),
            pltpu.VMEM((3, depth, perf_lanes), jnp.bfloat16),
            dma((4,)),
            dma((2, 5)),
            dma((2, 5)),
            dma((n_gy,)),
            dma((n_gy,)),
            dma((n_gx,)),
            dma((n_gx,)),
            dma((n_gx,)),
            dma((n_gx,)),
            dma((n_gy,)),
            dma((n_gy,)),
            dma((ks, groups)),
            dma((ks, groups)),
            dma((ks, groups)),
            dma((ks, groups)),
        ],
        compiler_params=pltpu.CompilerParams(collective_id=0, has_side_effects=True),
    )(
        grouped(adjoint_rhs),
        grouped(block_inverse),
        grouped(x_couplings),
        grouped(y_couplings),
        perf_cell.reshape(1, perfs),
        perf_well.reshape(1, perfs),
        perf_weight.reshape(1, perfs),
        well_adjoint,
    )
    return precond.reshape(adjoint_rhs.shape), update


def solution(mesh):
    placed = (
        P(None, None, "gx", "gy", None),
        P(None, None, "gx", "gy", None),
        P(None, None, "gx", "gy", None),
        P(None, None, "gx", "gy", None),
        P(("gx", "gy")),
        P(("gx", "gy")),
        P(("gx", "gy")),
        P(None, ("gx", "gy")),
    )
    return jax.shard_map(
        functools.partial(per_device, mesh.shape["gx"], mesh.shape["gy"]),
        mesh=mesh,
        in_specs=placed,
        out_specs=(P(None, None, "gx", "gy", None), P(None, ("gx", "gy"))),
        check_vma=False,
    )
```

```python
import functools

import jax
import jax.numpy as jnp
from jax import lax
from jax.experimental import pallas as pl
from jax.experimental.pallas import tpu as pltpu
from jax.sharding import PartitionSpec as P

MESH = pl.DeviceIdType.MESH
SUB = 8
LANES = 128


def round_up(value, step):
    return -(-value // step) * step


def dot_exact(values, hot, contract):
    rows = values.shape[0]
    high = values.astype(jnp.bfloat16)
    rest = values - high.astype(jnp.float32)
    middle = rest.astype(jnp.bfloat16)
    low = (rest - middle.astype(jnp.float32)).astype(jnp.bfloat16)
    dims = (((1,), (contract,)), ((), ()))
    return sum(
        lax.dot_general(part, hot, dims, preferred_element_type=jnp.float32)
        for part in (low, middle, high)
    )


def apply_inverse(inverse, values):
    comps = range(len(values))
    rows = []
    for c in comps:
        total = inverse[c][0] * values[0]
        for d in comps[1:]:
            total = total + inverse[c][d] * values[d]
        rows.append(total)
    return rows


def kernel(
    dims,
    rhs_h,
    inv_h,
    xc_h,
    yc_h,
    cell_ref,
    well_ref,
    weight_ref,
    adjoint_ref,
    out_ref,
    update_ref,
    rhs_s,
    inv_s,
    xc_s,
    yc_s,
    src_s,
    fwd_in,
    bwd_in,
    q_s,
    p_s,
    v_s,
    w_s,
    perf_s,
    ag1,
    ag2,
    rs1,
    rs2,
    well_hot,
    depth_hot,
    load_sem,
    halo_send,
    halo_recv,
    ag1_send,
    ag1_recv,
    ag2_send,
    ag2_recv,
    rs1_send,
    rs1_recv,
    rs2_send,
    rs2_recv,
    fwd_send,
    fwd_recv,
    bwd_send,
    bwd_recv,
):
    n_gx, n_gy, ks, comps, inner, margin, depth, perfs, own_wells = dims
    groups = inner + 2 * margin
    a = lax.axis_index("gx")
    b = lax.axis_index("gy")

    loads = [
        pltpu.make_async_copy(src, dst.at[:, :, pl.ds(margin, inner)], load_sem.at[n])
        for n, (src, dst) in enumerate(
            ((rhs_h, rhs_s), (inv_h, inv_s), (xc_h, xc_s), (yc_h, yc_s))
        )
    ]
    for copy in loads:
        copy.start()

    barrier = pltpu.get_barrier_semaphore()
    for d in range(1, n_gy):
        pl.semaphore_signal(
            barrier, inc=1, device_id=(a, lax.rem(b + d, n_gy)), device_id_type=MESH
        )
    for d in range(1, n_gx):
        pl.semaphore_signal(
            barrier, inc=1, device_id=(lax.rem(a + d, n_gx), b), device_id_type=MESH
        )

    lane = lax.broadcasted_iota(jnp.int32, (comps, ag1.shape[2]), 1)
    first_well = (a * n_gy + b) * own_wells
    tile = jnp.zeros((comps, ag1.shape[2]), jnp.float32)
    for w in range(own_wells):
        tile = jnp.where(lane == first_well + w, adjoint_ref[:, w : w + 1], tile)
    ag1[0] = jnp.zeros(ag1.shape[1:], jnp.float32)
    ag1[0, 0:comps] = tile
    perf_s[0] = jnp.zeros(perf_s.shape[1:], jnp.float32)
    perf_s[0, 0:1, 0:perfs] = cell_ref[...].astype(jnp.float32)
    perf_s[0, 1:2, 0:perfs] = well_ref[...].astype(jnp.float32)
    perf_s[0, 2:3, 0:perfs] = weight_ref[...]

    zero_edges = ((0, b == 0, 0), (1, b == n_gy - 1, margin + inner))
    for side, missing, start in zero_edges:

        @pl.when(missing)
        def _():
            perf_s[1 + side] = jnp.zeros(perf_s.shape[1:], jnp.float32)
            for ref in (rhs_s, inv_s, xc_s, yc_s):
                ref[:, :, start : start + margin] = jnp.zeros(
                    ref.shape[:2] + (margin,) + ref.shape[3:], jnp.float32
                )

    edge = jnp.zeros((ks, comps, SUB, depth), jnp.float32)
    w_s[:, 0] = edge
    w_s[:, groups + 1] = edge

    @pl.when(a == 0)
    def _():
        fwd_in[...] = jnp.zeros(fwd_in.shape, jnp.float32)

    pl.semaphore_wait(barrier, n_gy + n_gx - 2)

    def exchanged(src, dst, send, recv, axis):
        size = n_gy if axis else n_gx
        copies = []
        for d in range(1, size):
            target = (a, lax.rem(b + d, n_gy)) if axis else (lax.rem(a + d, n_gx), b)
            copies.append(
                pltpu.make_async_remote_copy(
                    src_ref=src,
                    dst_ref=dst.at[d],
                    send_sem=send.at[d],
                    recv_sem=recv.at[d],
                    device_id=target,
                    device_id_type=MESH,
                )
            )
        return copies

    def exchange(*args):
        copies = exchanged(*args)
        for copy in copies:
            copy.start()
        return copies

    first = exchange(ag1.at[0], ag1, ag1_send, ag1_recv, 1)

    def halo(side):
        target = (a, b + 1) if side == 0 else (a, b - 1)
        start = inner - margin if side == 0 else 0
        place = 0 if side == 0 else margin + inner
        pairs = [(perf_s.at[0], perf_s.at[1 + side])]
        for src, dst in ((inv_h, inv_s), (rhs_h, rhs_s), (xc_h, xc_s), (yc_h, yc_s)):
            pairs.append(
                (src.at[:, :, pl.ds(start, margin)], dst.at[:, :, pl.ds(place, margin)])
            )
        return [
            pltpu.make_async_remote_copy(
                src_ref=src,
                dst_ref=dst,
                send_sem=halo_send.at[side, n],
                recv_sem=halo_recv.at[side, n],
                device_id=target,
                device_id_type=MESH,
            )
            for n, (src, dst) in enumerate(pairs)
        ]

    sends = ((0, b < n_gy - 1), (1, b > 0))
    receives = ((0, b > 0), (1, b < n_gy - 1))
    def send_halo(chosen):
        for side, present in sends:

            @pl.when(chosen & present)
            def _():
                for copy in halo(side):
                    copy.start()

    send_halo(a == 0)

    width = perf_s.shape[2]
    well_count = ag1.shape[2]

    def perf_rows(slot):
        cell = perf_s[slot, 0:1].astype(jnp.int32)
        well = perf_s[slot, 1:2].astype(jnp.int32)
        line = lax.div(cell, depth)
        return line, cell - line * depth, well, perf_s[slot, 2:3]

    def make_hot(slot):
        _, place, well, _ = perf_rows(slot)
        ids = lax.broadcasted_iota(jnp.int32, (well_count, width), 0)
        well_hot[slot] = (ids == well).astype(jnp.float32).astype(jnp.bfloat16)
        ids = lax.broadcasted_iota(jnp.int32, (depth, width), 0)
        depth_hot[slot] = (ids == place).astype(jnp.float32).astype(jnp.bfloat16)

    make_hot(0)

    for copy in first:
        copy.wait_recv()
    row = ag1[0]
    for d in range(1, n_gy):
        row = row + ag1[d]
    ag2[0] = row
    second = exchange(ag2.at[0], ag2, ag2_send, ag2_recv, 0)
    send_halo(a > 0)

    for copy in loads:
        copy.wait()
    for side, present in receives:

        @pl.when(present)
        def _():
            for copy in halo(side):
                copy.wait_recv()

    make_hot(1)
    make_hot(2)
    for copy in second:
        copy.wait_recv()
    wells = ag2[0]
    for d in range(1, n_gx):
        wells = wells + ag2[d]

    for slot, count, skip, start in (
        (0, inner, 0, margin),
        (1, margin, (inner - margin) * SUB, 0),
        (2, margin, 0, margin + inner),
    ):
        line, _, _, weight = perf_rows(slot)
        picked = dot_exact(wells, well_hot[slot], 0)
        terms = picked * weight
        ids = lax.broadcasted_iota(jnp.int32, (count * SUB, width), 0) + skip
        hit = ids == line
        left = jnp.concatenate(
            [jnp.where(hit, terms[c : c + 1], 0.0) for c in range(comps)], axis=0
        )
        block = dot_exact(left, depth_hot[slot], 1)
        src_s[:, start : start + count] = block.reshape(comps, count, SUB, depth)

    sub = lax.broadcasted_iota(jnp.int32, (SUB, depth), 0)

    def load_inverse(g):
        return [[inv_s[c, d, g] for d in range(comps)] for c in range(comps)]

    def weigh(k, g, values):
        weighted = apply_inverse(load_inverse(g), values)
        for c in range(comps):
            v_s[k, g, c] = values[c]
            w_s[k, g + 1, c] = weighted[c]

    def solved(k, g):
        rest = []
        for c in range(comps):
            here = w_s[k, g + 1, c]
            below = jnp.where(
                sub == 0, pltpu.roll(w_s[k, g, c], 1, 0), pltpu.roll(here, 1, 0)
            )
            above = jnp.where(
                sub == SUB - 1,
                pltpu.roll(w_s[k, g + 2, c], SUB - 1, 0),
                pltpu.roll(here, SUB - 1, 0),
            )
            rest.append(v_s[k, g, c] - yc_s[0, c, g] * below - yc_s[1, c, g] * above)
        return apply_inverse(load_inverse(g), rest)

    def forward_copy(k, g):
        return pltpu.make_async_remote_copy(
            src_ref=q_s.at[k, g],
            dst_ref=fwd_in.at[k, g],
            send_sem=fwd_send.at[k, g],
            recv_sem=fwd_recv.at[k, g],
            device_id=(a + 1, b),
            device_id_type=MESH,
        )

    def backward_copy(k, g, src):
        return pltpu.make_async_remote_copy(
            src_ref=src.at[k, g],
            dst_ref=bwd_in.at[k, g],
            send_sem=bwd_send.at[k, g],
            recv_sem=bwd_recv.at[k, g],
            device_id=(a - 1, b),
            device_id_type=MESH,
        )

    def forward_first(k, g):
        @pl.when(a > 0)
        def _():
            forward_copy(k, g).wait_recv()

        weigh(
            k,
            g,
            [
                rhs_s[k, c, g] + src_s[c, g] - xc_s[0, c, g] * fwd_in[k, g, c]
                for c in range(comps)
            ],
        )

    def forward_second(k, g):
        result = solved(k, g)
        for c in range(comps):
            q_s[k, g, c] = result[c]

        @pl.when(a < n_gx - 1)
        def _():
            forward_copy(k, g).start()

        @pl.when(a == n_gx - 1)
        def _():
            backward_copy(k, g, q_s).start()

    def backward_first(k, g):
        backward_copy(k, g, p_s).wait_recv()
        weigh(k, g, [xc_s[1, c, g] * bwd_in[k, g, c] for c in range(comps)])

    def backward_second(k, g):
        result = solved(k, g)
        for c in range(comps):
            p_s[k, g, c] = q_s[k, g, c] - result[c]

        @pl.when(a > 0)
        def _():
            backward_copy(k, g, p_s).start()

    def march(k, opening, closing):
        opening(k, 0)

        def step(g, carry):
            opening(k, g)
            closing(k, g - 1)
            return carry

        lax.fori_loop(1, groups, step, 0)
        closing(k, groups - 1)

    def deliver(k, source):
        for c in range(comps):
            out_ref[k, c] = source[k, margin : margin + inner, c]

    def well_sums():
        line, _, _, weight = perf_rows(0)
        lines = inner * SUB
        final = out_ref[ks - 1].reshape(comps * lines, depth)
        columns = dot_exact(final, depth_hot[0], 0)
        ids = lax.broadcasted_iota(jnp.int32, (lines, width), 0)
        hit = ids == line
        sums = [
            jnp.sum(
                jnp.where(hit, columns[c * lines : (c + 1) * lines], 0.0),
                axis=0,
                keepdims=True,
            )
            * weight
            for c in range(comps)
        ]
        sums.append(jnp.zeros((SUB - comps, width), jnp.float32))
        rs1[0] = dot_exact(jnp.concatenate(sums, axis=0), well_hot[0], 1)
        for copy in exchanged(rs1.at[0], rs1, rs1_send, rs1_recv, 0):
            copy.start()

    order = range(ks - 1, -1, -1)
    for k in order:
        march(k, forward_first, forward_second)

    @pl.when(a == n_gx - 1)
    def _():
        for k in order:
            deliver(k, q_s)

    @pl.when(a < n_gx - 1)
    def _():
        march(ks - 1, backward_first, backward_second)
        deliver(ks - 1, p_s)

    @pl.when(a < n_gx - 1)
    def _():
        well_sums()

    @pl.when(a < n_gx - 1)
    def _():
        for k in order[1:]:
            march(k, backward_first, backward_second)
            deliver(k, p_s)

    @pl.when(a == n_gx - 1)
    def _():
        well_sums()

    third = exchanged(rs1.at[0], rs1, rs1_send, rs1_recv, 0)
    for copy in third:
        copy.wait_recv()
    column = rs1[0]
    for d in range(1, n_gx):
        column = column + rs1[d]
    rs2[0] = column
    fourth = exchange(rs2.at[0], rs2, rs2_send, rs2_recv, 1)

    for copy in first + second + third:
        copy.wait_send()
    for side, present in sends:

        @pl.when(present)
        def _():
            for copy in halo(side):
                copy.wait_send()

    def drain(make):
        for k in range(ks):

            def step(g, carry):
                make(k, g).wait_send()
                return carry

            lax.fori_loop(0, groups, step, 0)

    @pl.when(a < n_gx - 1)
    def _():
        drain(forward_copy)

    @pl.when(a > 0)
    def _():
        drain(lambda k, g: backward_copy(k, g, p_s))

    for copy in fourth:
        copy.wait()
    total = rs2[0]
    for d in range(1, n_gy):
        total = total + rs2[d]
    total = total[0:comps]
    picked = [
        jnp.sum(jnp.where(lane == first_well + w, total, 0.0), axis=1, keepdims=True)
        for w in range(own_wells)
    ]
    update_ref[...] = jnp.concatenate(picked, axis=1)


def per_device(
    n_gx,
    n_gy,
    adjoint_rhs,
    block_inverse,
    x_couplings,
    y_couplings,
    perf_cell,
    perf_well,
    perf_weight,
    well_adjoint,
):
    ks, comps, planes, lines, depth = adjoint_rhs.shape
    assert planes == 1 and n_gx > 1 and lines % SUB == 0
    inner = lines // SUB
    margin = round_up(2 * n_gx - 1, SUB) // SUB
    assert margin <= inner
    groups = inner + 2 * margin
    perfs = perf_cell.shape[0]
    own_wells = well_adjoint.shape[1]
    well_lanes = round_up(own_wells * n_gx * n_gy, LANES)
    perf_lanes = round_up(perfs, LANES)
    dims = (n_gx, n_gy, ks, comps, inner, margin, depth, perfs, own_wells)

    def grouped(array):
        return array.reshape(array.shape[:2] + (inner, SUB, depth))

    vmem = pl.BlockSpec(memory_space=pltpu.VMEM)
    hbm = pl.BlockSpec(memory_space=pl.ANY)
    f32 = jnp.float32
    dma = pltpu.SemaphoreType.DMA
    wide = lambda d0, d1: pltpu.VMEM((d0, d1, groups, SUB, depth), f32)
    flow = lambda extra: pltpu.VMEM((ks, groups + extra, comps, SUB, depth), f32)
    tiles = lambda count: pltpu.VMEM((count, SUB, well_lanes), f32)
    precond, update = pl.pallas_call(
        functools.partial(kernel, dims),
        out_shape=(
            pltpu.VMEM((ks, comps, inner, SUB, depth), f32),
            pltpu.VMEM((comps, own_wells), f32),
        ),
        in_specs=[hbm] * 4 + [vmem] * 4,
        out_specs=(vmem, vmem),
        scratch_shapes=[
            wide(ks, comps),
            wide(comps, comps),
            wide(2, comps),
            wide(2, comps),
            pltpu.VMEM((comps, groups, SUB, depth), f32),
            flow(0),
            flow(0),
            flow(0),
            flow(0),
            flow(0),
            flow(2),
            pltpu.VMEM((3, SUB, perf_lanes), f32),
            tiles(n_gy),
            tiles(n_gx),
            tiles(n_gx),
            tiles(n_gy),
            pltpu.VMEM((3, well_lanes, perf_lanes), jnp.bfloat16),
            pltpu.VMEM((3, depth, perf_lanes), jnp.bfloat16),
            dma((4,)),
            dma((2, 5)),
            dma((2, 5)),
            dma((n_gy,)),
            dma((n_gy,)),
            dma((n_gx,)),
            dma((n_gx,)),
            dma((n_gx,)),
            dma((n_gx,)),
            dma((n_gy,)),
            dma((n_gy,)),
            dma((ks, groups)),
            dma((ks, groups)),
            dma((ks, groups)),
            dma((ks, groups)),
        ],
        compiler_params=pltpu.CompilerParams(collective_id=0, has_side_effects=True),
    )(
        grouped(adjoint_rhs),
        grouped(block_inverse),
        grouped(x_couplings),
        grouped(y_couplings),
        perf_cell.reshape(1, perfs),
        perf_well.reshape(1, perfs),
        perf_weight.reshape(1, perfs),
        well_adjoint,
    )
    return precond.reshape(adjoint_rhs.shape), update


def solution(mesh):
    placed = (
        P(None, None, "gx", "gy", None),
        P(None, None, "gx", "gy", None),
        P(None, None, "gx", "gy", None),
        P(None, None, "gx", "gy", None),
        P(("gx", "gy")),
        P(("gx", "gy")),
        P(("gx", "gy")),
        P(None, ("gx", "gy")),
    )
    return jax.shard_map(
        functools.partial(per_device, mesh.shape["gx"], mesh.shape["gy"]),
        mesh=mesh,
        in_specs=placed,
        out_specs=(P(None, None, "gx", "gy", None), P(None, ("gx", "gy"))),
        check_vma=False,
    )
```
